32 devices in a mesh: blk: 4 (over z), virt: 8 (over y, x, core).
Axes of the slice: x: 2, y: 2, z: 4, core: 2. Of those that a mesh axis runs over, the one named last changes fastest.
Arguments:
- integrals: bfloat16 [512, 16, 4096], P(('blk', 'virt')), may hold values from -0.09375 to 0.09375
- amplitudes: bfloat16 [256, 4096], P('blk'), may hold values from -6 to 6
- readers: int32 [512], P(('blk', 'virt')), may hold values from 0 to 7, as said below
- row_slots: int32 [512], P(('blk', 'virt')), may hold values from 0 to 3
- tile_mask: int32 [512, 4], P(('blk', 'virt')), may hold values 0 or 1
- virt_energy: float32 [2048], P(('blk', 'virt')), may hold values from 1 to 3
- occ_energy: float32 [1200], replicated, may hold values from -1 to -0.25
- pair_first: int32 [256], replicated, may hold values from 0 to 1199
- pair_second: int32 [256], replicated, may hold values from 0 to 1199
Outputs:
- update: bfloat16 [2048, 256], P(('blk', 'virt'))
The draws below stay inside these ranges and needn't reach their ends.
Inputs may be any that keep to these rules, and one draw needn't show every extreme that they name: `readers`: each tile names a reader on the virt axis in the same blk row as its generating device; one device names one reader at most 4 times, and in every blk row some reader is named 4 times by every device of that row.
All inputs are finite; a program needn't handle non-finite values. No bound on the sum of `tile_mask` on one device may be relied on, other than what follows from the above.
Results may differ from the reference program's by a relative error of at most 0.001.
Values may be sent and summed in bfloat16 or wider, within the bound.
A program may use at most 64 MiB of HBM per device.

```python
import jax
import jax.numpy as jnp
from jax import lax

TW = 4096
NOCC = 1200
TR = 16
GEN = 16
RB_DEV = 4
OPB = 64
TILES = 512
IJ = 256
ROWS = 2048
N_BLK = 4
N_VIRT = 8


def draw_readers(key, part):
    capacity = max(1, 2 * GEN // N_VIRT)
    slot_count = N_VIRT * capacity
    key_hot = jax.random.fold_in(key, 11)
    key_pref = jax.random.fold_in(key, 12)
    key_jitter = jax.random.fold_in(key, 13)
    hot_reader = jax.random.randint(key_hot, (N_BLK,), 0, N_VIRT)
    preference = jax.random.randint(key_pref, (N_BLK, N_VIRT), 0, 4)
    preference = jnp.where(jnp.arange(N_VIRT)[None, :] == hot_reader[:, None], 16, preference)
    device_pref = jnp.repeat(preference, N_VIRT, axis=0)
    slot_pref = jnp.repeat(device_pref, capacity, axis=1)
    jitter_values = jax.random.randint(key_jitter, (N_BLK * N_VIRT, slot_count), 0, 65536)
    scores = (slot_pref * 32768 + jitter_values) * slot_count + jnp.arange(slot_count)[None, :]
    ranking = jnp.argsort(-scores, axis=1)[:, :GEN]
    chosen = ranking // capacity
    return chosen.reshape(-1).astype(jnp.int32)


def touch_ends(entries, rng, least, top_value):
    shape = entries.shape
    place = [jax.random.randint(jax.random.fold_in(rng, axis), (), 0, shape[axis]) for axis in range(len(shape))]
    entries = entries.at[tuple(place)].set(least)
    longest = shape.index(max(shape))
    place[longest] = (place[longest] + 1) % shape[longest]
    return entries.at[tuple(place)].set(top_value)


def levels(key, extent, cuts, least, high):
    factor_of = 1.0
    for position, blocks in cuts:
        heights = jax.random.uniform(jax.random.fold_in(jax.random.fold_in(key, 6), position), (blocks,), jnp.float32, least / len(cuts), high / len(cuts))
        factor_of = factor_of * jnp.repeat(jnp.exp(heights), extent[position] // blocks).reshape((-1,) + (1,) * (len(extent) - 1 - position))
    return factor_of


def centred(own_key, extent, scale, reach, split=(), kind=jnp.bfloat16):
    drawn = scale * jax.random.normal(own_key, extent, jnp.float32)
    if split:
        drawn = drawn * levels(own_key, extent, split, -0.22, 0.18)
    return jnp.clip(drawn, -reach, reach).astype(kind)


def setup_inputs(seed: int = 0) -> dict:
    streams_of = jax.random.split(jax.random.key(seed), 10)
    integrals = centred(streams_of[0], (TILES, TR, TW), TW ** -0.5, 0.09375, ((0, 32),))
    amplitudes = centred(streams_of[1], (IJ, TW), 1.0, 6.0, ((0, 4),))
    readers = draw_readers(jax.random.fold_in(streams_of[9], 71), 0)
    row_slots = touch_ends(jax.random.randint(streams_of[3], (TILES,), 0, RB_DEV), jax.random.fold_in(streams_of[3], 1), 0, RB_DEV - 1).astype(jnp.int32)
    tile_mask = touch_ends((jax.random.randint(streams_of[4], (TILES, N_BLK), 0, 2) < 1).astype(jnp.int32), jax.random.fold_in(streams_of[4], 1), 0, 1)
    virt_energy = jnp.clip(1.0 + 2.0 * jax.random.uniform(streams_of[5], (ROWS,), jnp.float32) ** levels(streams_of[5], (ROWS,), ((0, 32),), -0.2, 0.2), 1.0, 3.0)
    occ_energy = jnp.clip(jax.random.uniform(streams_of[6], (NOCC,), jnp.float32, -1.0, -0.25), -1.0, -0.25)
    pair_first = touch_ends(jax.random.randint(streams_of[7], (IJ,), 0, NOCC), jax.random.fold_in(streams_of[7], 1), 0, NOCC - 1).astype(jnp.int32)
    pair_second = touch_ends(jax.random.randint(streams_of[8], (IJ,), 0, NOCC), jax.random.fold_in(streams_of[8], 1), 0, NOCC - 1).astype(jnp.int32)
    return dict(integrals=integrals, amplitudes=amplitudes, readers=readers, row_slots=row_slots, tile_mask=tile_mask, virt_energy=virt_energy, occ_energy=occ_energy, pair_first=pair_first, pair_second=pair_second)


def reference(integrals, amplitudes, readers, row_slots, tile_mask, virt_energy, occ_energy, pair_first, pair_second):
    devices = N_BLK * N_VIRT
    rows_dev = RB_DEV * TR
    amps_float = amplitudes.astype(jnp.float32)
    tile_array = integrals.reshape(devices, GEN, TR, TW)
    dest_all = readers.reshape(devices, GEN)
    slot_all = row_slots.reshape(devices, GEN)
    mask_all = tile_mask.reshape(devices, GEN, N_BLK)

    def accumulate(running, inputs):
        source, tile_block, dest_now, slot_now, mask_now = inputs
        product = jnp.einsum('gtw,pw->gtp', tile_block.astype(jnp.float32), amps_float,
                             precision=lax.Precision.HIGHEST)
        weight = jnp.repeat(mask_now.astype(jnp.float32), OPB, axis=1)
        product = product * weight[:, None, :]
        first_row = ((source // N_VIRT) * N_VIRT + dest_now) * rows_dev + slot_now * TR
        row_index = (first_row[:, None] + jnp.arange(TR, dtype=jnp.int32)[None, :]).astype(jnp.int32)
        running = running.at[row_index.reshape(-1)].add(product.reshape(GEN * TR, IJ))
        return running, None

    summed, _ = lax.scan(accumulate, jnp.zeros((ROWS, IJ), jnp.float32),
                         (jnp.arange(devices, dtype=jnp.int32), tile_array, dest_all, slot_all, mask_all))
    denominator = virt_energy[:, None] - occ_energy[pair_first][None, :] - occ_energy[pair_second][None, :]
    return (summed / denominator).astype(jnp.bfloat16)
```

```python
import functools

import jax
import jax.numpy as jnp
from jax import lax
from jax.experimental import pallas as pl
from jax.experimental.pallas import tpu as pltpu
from jax.sharding import PartitionSpec as P

MESH = pl.DeviceIdType.MESH


def flip(index, bits):
    step = 1
    while step <= bits:
        if bits & step:
            index = index + step * (1 - 2 * ((index // step) % 2))
        step *= 2
    return index


def panel_order(blk_count):
    order = [0, 3, 2, 1] if blk_count >= 4 else [0, 1]
    return order + list(range(4, blk_count))


def kernel(
    blk_count,
    virt_count,
    chunks,
    tiles_hbm,
    amp_hbm,
    readers_hbm,
    slots_hbm,
    mask_hbm,
    virt_hbm,
    occ_hbm,
    first_hbm,
    second_hbm,
    out_ref,
    tiles,
    amp,
    products,
    weights,
    goals,
    hot,
    partial,
    landed,
    denominator,
    readers,
    slots,
    mask,
    virt_energy,
    occ,
    first,
    second,
    local_sem,
    swap_send,
    swap_recv,
    far_send,
    far_recv,
    near_send,
    near_recv,
    plane_send,
    plane_recv,
    sum_send,
    sum_recv,
):
    b = lax.axis_index("blk")
    v = lax.axis_index("virt")
    core = v % 2
    spot = (v // 2) % 4
    generated = readers.shape[0]
    lanes = tiles.shape[0] // 2
    tile_rows = lanes // generated
    panel_rows, width = amp_hbm.shape
    share = panel_rows // 2
    rows = out_ref.shape[0]
    row_blocks = rows // tile_rows
    order = panel_order(blk_count)
    groups = blk_count // 2
    group_width = 2 * share
    packed_width = 2 * group_width
    packed_rows = rows // 2
    quarter = width // 4
    chunk = quarter // chunks
    sibling = (b, flip(v, 1))

    def keep(d):
        return pl.ds(order.index(d) * share, share)

    mine = pl.ds(pl.multiple_of(core * share, share), share)
    locals_ = [
        pltpu.make_async_copy(source, target, local_sem.at[index])
        for index, (source, target) in enumerate(
            (
                (readers_hbm, readers),
                (slots_hbm, slots),
                (mask_hbm, mask),
                (virt_hbm, virt_energy),
                (occ_hbm, occ),
                (first_hbm, first),
                (second_hbm, second),
                (amp_hbm.at[mine], amp.at[keep(0)]),
                (tiles_hbm, tiles.at[pl.ds(0, lanes)]),
            )
        )
    ]

    barrier = pltpu.get_barrier_semaphore()
    for d in range(1, blk_count):
        pl.semaphore_signal(barrier, inc=1, device_id=(flip(b, d), v), device_id_type=MESH)
    for d in range(1, virt_count):
        pl.semaphore_signal(barrier, inc=1, device_id=(b, flip(v, d)), device_id_type=MESH)
    for copy in locals_:
        copy.start()
    pl.semaphore_wait(barrier, blk_count + virt_count - 2)

    started = []

    def send(source, target, send_sem, recv_sem, device):
        copy = pltpu.make_async_remote_copy(
            source, target, send_sem, recv_sem, device_id=device, device_id_type=MESH
        )
        copy.start()
        started.append(copy)
        return copy

    def columns(spot_now, start, size):
        return pl.ds(pl.multiple_of(spot_now * quarter + start, size), size)

    far = {}
    for d in order[1:3] + order[4:]:
        if d == 1:
            continue
        for j in range(chunks):
            area = columns(spot, j * chunk, chunk)
            far[d, j] = send(
                amp_hbm.at[mine, area],
                amp.at[keep(d), area],
                far_send.at[d, j],
                far_recv.at[d, j],
                (flip(b, d), v),
            )
    near = {}
    for step in range(4):
        area = columns(flip(spot, step), 0, quarter)
        near[step] = send(
            amp_hbm.at[mine, area],
            amp.at[keep(1), area],
            near_send.at[step],
            near_recv.at[step],
            (flip(b, 1), v),
        )
    tiles_swap = send(
        tiles_hbm, tiles.at[pl.ds(lanes, lanes)], swap_send.at[0], swap_recv.at[0], sibling
    )

    for copy in locals_[:7]:
        copy.wait()
    lane = lax.broadcasted_iota(jnp.int32, (1, lanes), 1)
    goal = jnp.zeros((1, lanes), jnp.int32)
    half_blocks = row_blocks // 2
    hot_rows = virt_count * packed_rows
    for t in range(generated):
        place = (
            (slots[t] // half_blocks) * hot_rows
            + readers[t] * packed_rows
            + (slots[t] % half_blocks) * tile_rows
        )
        goal = jnp.where(lane // tile_rows == t, place, goal)
    goal = goal + lane % tile_rows
    goals[0] = jnp.broadcast_to(goal, goals.shape[1:])
    goals_swap = send(goals.at[0], goals.at[1], swap_send.at[1], swap_recv.at[1], sibling)

    packed_lane = lax.broadcasted_iota(jnp.int32, (1, packed_width), 1)
    for g in range(groups):
        one, two = flip(b, order[2 * g]), flip(b, order[2 * g + 1])
        weights[g, :lanes] = jnp.concatenate(
            [
                jnp.broadcast_to(
                    jnp.where(packed_lane % group_width < share, mask[one, t], mask[two, t]).astype(
                        jnp.float32
                    ),
                    (tile_rows, packed_width),
                )
                for t in range(generated)
            ],
            axis=0,
        )
    weights_swap = send(
        weights.at[:, pl.ds(0, lanes)],
        weights.at[:, pl.ds(lanes, lanes)],
        swap_send.at[2],
        swap_recv.at[2],
        sibling,
    )

    def mark(part):
        row = lax.broadcasted_iota(jnp.int32, (2 * hot_rows, lanes), 0)
        hot[:, pl.ds(part * lanes, lanes)] = (
            (row == goals[part][0:1]).astype(jnp.float32).astype(jnp.bfloat16)
        )

    def energies():
        levels = occ.shape[0]
        occ_row = occ[...].reshape(1, levels)
        occ_high = occ_row.astype(jnp.bfloat16).astype(jnp.float32)
        occ_rest = occ_row - occ_high
        occ_mid = occ_rest.astype(jnp.bfloat16).astype(jnp.float32)
        occ_low = occ_rest - occ_mid
        term = lax.broadcasted_iota(jnp.int32, (8, levels), 0)
        occ_terms = jnp.where(
            term == 0, occ_high, jnp.where(term == 1, occ_mid, jnp.where(term == 2, occ_low, 0.0))
        ).astype(jnp.bfloat16)
        count = first.shape[1]
        level = lax.broadcasted_iota(jnp.int32, (levels, count), 0)

        def energy(pair_ref):
            chosen = (level == pair_ref[...]).astype(jnp.float32).astype(jnp.bfloat16)
            terms = jnp.dot(occ_terms, chosen, preferred_element_type=jnp.float32)
            return (terms[0:1] + terms[1:2]) + terms[2:3]

        diagonal = lax.broadcasted_iota(jnp.int32, (rows, rows), 0) == lax.broadcasted_iota(
            jnp.int32, (rows, rows), 1
        )
        virt_column = jnp.sum(jnp.where(diagonal, virt_energy[...], 0.0), axis=1, keepdims=True)
        denominator[...] = (virt_column - energy(first)) - energy(second)

    plane = {}

    def forward(d):
        for j in range(chunks):
            far[d, j].wait_recv()
            area = amp.at[keep(d), columns(spot, j * chunk, chunk)]
            for bits in (3, 1, 2):
                plane[d, bits, j] = send(
                    area,
                    area,
                    plane_send.at[d, bits, j],
                    plane_recv.at[d, bits, j],
                    (b, flip(v, 2 * bits)),
                )

    def multiply(g, step):
        for d in order[2 * g : 2 * g + 2]:
            if d == 1:
                near[step].wait_recv()
            elif d and step:
                for j in range(chunks):
                    plane[d, step, j].wait_recv()
        depth = columns(flip(spot, step), 0, quarter)
        term = lax.dot_general(
            tiles[:, depth],
            amp[pl.ds(g * group_width, group_width), depth],
            (((1,), (1,)), ((), ())),
            preferred_element_type=jnp.float32,
        )
        products[g] = term if step == 0 else products[g] + term

    sums = {}

    def contract(g):
        product = products[g]
        product = jnp.concatenate([product, product], axis=1) * weights[g]
        both = None
        for half in range(2):
            part = jnp.where(packed_lane // group_width == half, product, 0.0)
            high = part.astype(jnp.bfloat16)
            low = (part - high.astype(jnp.float32)).astype(jnp.bfloat16)
            term = jnp.dot(
                hot[pl.ds(half * hot_rows, hot_rows)],
                jnp.concatenate([high, low], axis=1),
                preferred_element_type=jnp.float32,
            )
            both = term if both is None else both + term
        partial[g] = both[:, :packed_width] + both[:, packed_width:]
        for d in [6, 7, 2, 3, 4, 5] + list(range(8, virt_count)) + [1]:
            peer = flip(v, d)
            sums[g, d] = send(
                partial.at[g, pl.ds(pl.multiple_of(peer * packed_rows, packed_rows), packed_rows)],
                landed.at[g, d],
                sum_send.at[g, d],
                sum_recv.at[g, d],
                (b, peer),
            )

    mark(0)
    if blk_count >= 4:
        forward(3)
    goals_swap.wait_recv()
    mark(1)
    if blk_count >= 4:
        forward(2)
    energies()
    locals_[7].wait()
    locals_[8].wait()
    tiles_swap.wait_recv()
    weights_swap.wait_recv()
    for g in range(groups):
        if g >= 2:
            forward(order[2 * g])
            forward(order[2 * g + 1])
        for step in range(4):
            multiply(g, step)
        contract(g)

    blocks = {}
    for g in range(groups):
        own = pl.ds(pl.multiple_of(v * packed_rows, packed_rows), packed_rows)
        same, other = partial[g, own, :], None
        for d in range(1, virt_count):
            sums[g, d].wait_recv()
            if d % 2 == 0:
                same = same + landed[g, d]
            else:
                other = landed[g, d] if other is None else other + landed[g, d]
        low_core = jnp.where(core == 0, same, other)
        high_core = jnp.where(core == 0, other, same)
        for i in range(2):
            blocks[order[2 * g + i]] = jnp.concatenate(
                [
                    jnp.concatenate(
                        [
                            part[:, half * group_width + i * share :][:, :share]
                            for part in (low_core, high_core)
                        ],
                        axis=1,
                    )
                    for half in range(2)
                ],
                axis=0,
            )
    step = 1
    while step < blk_count:
        odd = (b // step) % 2 == 1
        blocks = {d: jnp.where(odd, blocks[d ^ step], blocks[d]) for d in blocks}
        step *= 2
    total = jnp.concatenate([blocks[d] for d in range(blk_count)], axis=1)
    out_ref[...] = (total / denominator[...]).astype(out_ref.dtype)

    for copy in started:
        copy.wait_send()


def body(
    blk_count,
    virt_count,
    integrals,
    amplitudes,
    readers,
    row_slots,
    tile_mask,
    virt_energy,
    occ_energy,
    pair_first,
    pair_second,
):
    generated, tile_rows, width = integrals.shape
    panel_rows = amplitudes.shape[0]
    rows = virt_energy.shape[0]
    columns = blk_count * panel_rows
    groups = blk_count // 2
    levels = occ_energy.shape[0]
    lanes = generated * tile_rows
    packed_rows = rows // 2
    packed_width = 2 * panel_rows
    chunks = 2
    anywhere = pl.BlockSpec(memory_space=pl.ANY)
    return pl.pallas_call(
        functools.partial(kernel, blk_count, virt_count, chunks),
        out_shape=jax.ShapeDtypeStruct((rows, columns), jnp.bfloat16),
        in_specs=[anywhere] * 9,
        out_specs=pl.BlockSpec(memory_space=pltpu.VMEM),
        scratch_shapes=[
            pltpu.VMEM((2 * lanes, width), jnp.bfloat16),
            pltpu.VMEM((columns // 2, width), jnp.bfloat16),
            pltpu.VMEM((groups, 2 * lanes, panel_rows), jnp.float32),
            pltpu.VMEM((groups, 2 * lanes, packed_width), jnp.float32),
            pltpu.VMEM((2, 8, lanes), jnp.int32),
            pltpu.VMEM((virt_count * rows, 2 * lanes), jnp.bfloat16),
            pltpu.VMEM((groups, virt_count * packed_rows, packed_width), jnp.float32),
            pltpu.VMEM((groups, virt_count, packed_rows, packed_width), jnp.float32),
            pltpu.VMEM((rows, columns), jnp.float32),
            pltpu.SMEM((generated,), jnp.int32),
            pltpu.SMEM((generated,), jnp.int32),
            pltpu.SMEM((blk_count, generated), jnp.int32),
            pltpu.VMEM((1, rows), jnp.float32),
            pltpu.VMEM((levels,), jnp.float32),
            pltpu.VMEM((1, columns), jnp.int32),
            pltpu.VMEM((1, columns), jnp.int32),
            pltpu.SemaphoreType.DMA((9,)),
            pltpu.SemaphoreType.DMA((3,)),
            pltpu.SemaphoreType.DMA((3,)),
            pltpu.SemaphoreType.DMA((blk_count, chunks)),
            pltpu.SemaphoreType.DMA((blk_count, chunks)),
            pltpu.SemaphoreType.DMA((4,)),
            pltpu.SemaphoreType.DMA((4,)),
            pltpu.SemaphoreType.DMA((blk_count, 4, chunks)),
            pltpu.SemaphoreType.DMA((blk_count, 4, chunks)),
            pltpu.SemaphoreType.DMA((groups, virt_count)),
            pltpu.SemaphoreType.DMA((groups, virt_count)),
        ],
        compiler_params=pltpu.CompilerParams(
            collective_id=0, has_side_effects=True, vmem_limit_bytes=60 * 1024 * 1024
        ),
        name="ladder",
    )(
        integrals.reshape(generated * tile_rows, width),
        amplitudes,
        readers,
        row_slots,
        tile_mask.T,
        virt_energy.reshape(1, rows),
        occ_energy,
        pair_first.reshape(1, columns),
        pair_second.reshape(1, columns),
    )


def solution(mesh):
    placed = (
        P(("blk", "virt"), None, None),
        P("blk", None),
        P(("blk", "virt")),
        P(("blk", "virt")),
        P(("blk", "virt"), None),
        P(("blk", "virt")),
        P(),
        P(),
        P(),
    )
    return jax.shard_map(
        functools.partial(body, mesh.shape["blk"], mesh.shape["virt"]),
        mesh=mesh,
        in_specs=placed,
        out_specs=P(("blk", "virt"), None),
        check_vma=False,
    )
```

```python
import functools

import jax
import jax.numpy as jnp
from jax import lax
from jax.experimental import pallas as pl
from jax.experimental.pallas import tpu as pltpu
from jax.sharding import PartitionSpec as P

MESH = pl.DeviceIdType.MESH


def flip(index, bits):
    step = 1
    while step <= bits:
        if bits & step:
            index = index + step * (1 - 2 * ((index // step) % 2))
        step *= 2
    return index


def panel_order(blk_count):
    order = [0, 3, 2, 1] if blk_count >= 4 else [0, 1]
    return order + list(range(4, blk_count))


def kernel(
    blk_count,
    virt_count,
    chunks,
    tiles_hbm,
    amp_hbm,
    readers_hbm,
    slots_hbm,
    mask_hbm,
    virt_hbm,
    occ_hbm,
    first_hbm,
    second_hbm,
    out_ref,
    tiles,
    amp,
    products,
    weights,
    goals,
    hot,
    partial,
    landed,
    denominator,
    readers,
    slots,
    mask,
    virt_energy,
    occ,
    first,
    second,
    local_sem,
    swap_send,
    swap_recv,
    far_send,
    far_recv,
    near_send,
    near_recv,
    plane_send,
    plane_recv,
    sum_send,
    sum_recv,
):
    b = lax.axis_index("blk")
    v = lax.axis_index("virt")
    core = v % 2
    spot = (v // 2) % 4
    generated = readers.shape[0]
    lanes = tiles.shape[0] // 2
    tile_rows = lanes // generated
    panel_rows, width = amp_hbm.shape
    share = panel_rows // 2
    rows = out_ref.shape[0]
    row_blocks = rows // tile_rows
    order = panel_order(blk_count)
    groups = blk_count // 2
    group_width = 2 * share
    packed_width = 2 * group_width
    packed_rows = rows // 2
    quarter = width // 4
    chunk = quarter // chunks
    sibling = (b, flip(v, 1))

    def keep(d):
        return pl.ds(order.index(d) * share, share)

    mine = pl.ds(pl.multiple_of(core * share, share), share)
    locals_ = [
        pltpu.make_async_copy(source, target, local_sem.at[index])
        for index, (source, target) in enumerate(
            (
                (readers_hbm, readers),
                (slots_hbm, slots),
                (mask_hbm, mask),
                (virt_hbm, virt_energy),
                (occ_hbm, occ),
                (first_hbm, first),
                (second_hbm, second),
                (amp_hbm.at[mine], amp.at[keep(0)]),
                (tiles_hbm, tiles.at[pl.ds(0, lanes)]),
            )
        )
    ]

    barrier = pltpu.get_barrier_semaphore()
    for d in range(1, blk_count):
        pl.semaphore_signal(barrier, inc=1, device_id=(flip(b, d), v), device_id_type=MESH)
    for d in range(1, virt_count):
        pl.semaphore_signal(barrier, inc=1, device_id=(b, flip(v, d)), device_id_type=MESH)
    for copy in locals_:
        copy.start()
    pl.semaphore_wait(barrier, blk_count + virt_count - 2)

    started = []

    def send(source, target, send_sem, recv_sem, device):
        copy = pltpu.make_async_remote_copy(
            source, target, send_sem, recv_sem, device_id=device, device_id_type=MESH
        )
        copy.start()
        started.append(copy)
        return copy

    def columns(spot_now, start, size):
        return pl.ds(pl.multiple_of(spot_now * quarter + start, size), size)

    far = {}
    for d in order[1:3] + order[4:]:
        if d == 1:
            continue
        for j in range(chunks):
            area = columns(spot, j * chunk, chunk)
            far[d, j] = send(
                amp_hbm.at[mine, area],
                amp.at[keep(d), area],
                far_send.at[d, j],
                far_recv.at[d, j],
                (flip(b, d), v),
            )
    near = {}
    for step in range(2):
        area = pl.ds(pl.multiple_of(flip(spot // 2, step) * 2 * quarter, quarter), 2 * quarter)
        near[step] = send(
            amp_hbm.at[mine, area],
            amp.at[keep(1), area],
            near_send.at[step],
            near_recv.at[step],
            (flip(b, 1), v),
        )
    tiles_swap = send(
        tiles_hbm, tiles.at[pl.ds(lanes, lanes)], swap_send.at[0], swap_recv.at[0], sibling
    )

    for copy in locals_[:7]:
        copy.wait()
    lane = lax.broadcasted_iota(jnp.int32, (1, lanes), 1)
    goal = jnp.zeros((1, lanes), jnp.int32)
    half_blocks = row_blocks // 2
    hot_rows = virt_count * packed_rows
    for t in range(generated):
        place = (
            (slots[t] // half_blocks) * hot_rows
            + readers[t] * packed_rows
            + (slots[t] % half_blocks) * tile_rows
        )
        goal = jnp.where(lane // tile_rows == t, place, goal)
    goal = goal + lane % tile_rows
    goals[0] = jnp.broadcast_to(goal, goals.shape[1:])
    goals_swap = send(goals.at[0], goals.at[1], swap_send.at[1], swap_recv.at[1], sibling)

    packed_lane = lax.broadcasted_iota(jnp.int32, (1, packed_width), 1)
    for g in range(groups):
        one, two = flip(b, order[2 * g]), flip(b, order[2 * g + 1])
        weights[g, :lanes] = jnp.concatenate(
            [
                jnp.broadcast_to(
                    jnp.where(packed_lane % group_width < share, mask[one, t], mask[two, t]).astype(
                        jnp.float32
                    ),
                    (tile_rows, packed_width),
                )
                for t in range(generated)
            ],
            axis=0,
        )
    weights_swap = send(
        weights.at[:, pl.ds(0, lanes)],
        weights.at[:, pl.ds(lanes, lanes)],
        swap_send.at[2],
        swap_recv.at[2],
        sibling,
    )

    def mark(part):
        row = lax.broadcasted_iota(jnp.int32, (2 * hot_rows, lanes), 0)
        hot[:, pl.ds(part * lanes, lanes)] = (
            (row == goals[part][0:1]).astype(jnp.float32).astype(jnp.bfloat16)
        )

    def energies():
        levels = occ.shape[0]
        occ_row = occ[...].reshape(1, levels)
        occ_high = occ_row.astype(jnp.bfloat16).astype(jnp.float32)
        occ_rest = occ_row - occ_high
        occ_mid = occ_rest.astype(jnp.bfloat16).astype(jnp.float32)
        occ_low = occ_rest - occ_mid
        term = lax.broadcasted_iota(jnp.int32, (8, levels), 0)
        occ_terms = jnp.where(
            term == 0, occ_high, jnp.where(term == 1, occ_mid, jnp.where(term == 2, occ_low, 0.0))
        ).astype(jnp.bfloat16)
        count = first.shape[1]
        level = lax.broadcasted_iota(jnp.int32, (levels, count), 0)

        def energy(pair_ref):
            chosen = (level == pair_ref[...]).astype(jnp.float32).astype(jnp.bfloat16)
            terms = jnp.dot(occ_terms, chosen, preferred_element_type=jnp.float32)
            return (terms[0:1] + terms[1:2]) + terms[2:3]

        diagonal = lax.broadcasted_iota(jnp.int32, (rows, rows), 0) == lax.broadcasted_iota(
            jnp.int32, (rows, rows), 1
        )
        virt_column = jnp.sum(jnp.where(diagonal, virt_energy[...], 0.0), axis=1, keepdims=True)
        denominator[...] = (virt_column - energy(first)) - energy(second)

    plane = {}

    def forward(d):
        for j in range(chunks):
            far[d, j].wait_recv()
            area = amp.at[keep(d), columns(spot, j * chunk, chunk)]
            for bits in (3, 1, 2):
                plane[d, bits, j] = send(
                    area,
                    area,
                    plane_send.at[d, bits, j],
                    plane_recv.at[d, bits, j],
                    (b, flip(v, 2 * bits)),
                )

    def multiply(g, step, parts=None):
        for j in range(chunks) if parts is None else parts:
            for d in order[2 * g : 2 * g + 2]:
                if d == 1 and step % 2 == 0 and j == 0:
                    near[step // 2].wait_recv()
                elif d > 1 and step:
                    plane[d, step, j].wait_recv()
        size = quarter if parts is None else chunk * len(parts)
        depth = columns(flip(spot, step), 0 if parts is None else parts[0] * chunk, size)
        term = lax.dot_general(
            tiles[:, depth],
            amp[pl.ds(g * group_width, group_width), depth],
            (((1,), (1,)), ((), ())),
            preferred_element_type=jnp.float32,
        )
        products[g] = term if step == 0 and (parts is None or parts[0] == 0) else products[g] + term

    sums = {}

    def contract(g):
        product = products[g]
        product = jnp.concatenate([product, product], axis=1) * weights[g]
        both = None
        for half in range(2):
            part = jnp.where(packed_lane // group_width == half, product, 0.0)
            high = part.astype(jnp.bfloat16)
            low = (part - high.astype(jnp.float32)).astype(jnp.bfloat16)
            term = jnp.dot(
                hot[pl.ds(half * hot_rows, hot_rows)],
                jnp.concatenate([high, low], axis=1),
                preferred_element_type=jnp.float32,
            )
            both = term if both is None else both + term
        partial[g] = both[:, :packed_width] + both[:, packed_width:]
        for d in [6, 7, 2, 3, 4, 5] + list(range(8, virt_count)) + [1]:
            peer = flip(v, d)
            sums[g, d] = send(
                partial.at[g, pl.ds(pl.multiple_of(peer * packed_rows, packed_rows), packed_rows)],
                landed.at[g, d],
                sum_send.at[g, d],
                sum_recv.at[g, d],
                (b, peer),
            )

    mark(0)
    if blk_count >= 4:
        forward(3)
    goals_swap.wait_recv()
    mark(1)
    locals_[7].wait()
    locals_[8].wait()
    tiles_swap.wait_recv()
    multiply(0, 0)
    if blk_count >= 4:
        forward(2)
        multiply(1, 0)
    for step in range(1, 4):
        multiply(0, step)
    weights_swap.wait_recv()
    contract(0)
    energies()
    for g in range(1, groups):
        if g >= 2:
            forward(order[2 * g])
            forward(order[2 * g + 1])
            multiply(g, 0)
        for j in range(chunks):
            for step in range(1, 4):
                multiply(g, step, [j])
        contract(g)

    blocks = {}
    for g in range(groups):
        own = pl.ds(pl.multiple_of(v * packed_rows, packed_rows), packed_rows)
        same, other = partial[g, own, :], None
        for d in range(1, virt_count):
            sums[g, d].wait_recv()
            if d % 2 == 0:
                same = same + landed[g, d]
            else:
                other = landed[g, d] if other is None else other + landed[g, d]
        low_core = jnp.where(core == 0, same, other)
        high_core = jnp.where(core == 0, other, same)
        for i in range(2):
            blocks[order[2 * g + i]] = jnp.concatenate(
                [
                    jnp.concatenate(
                        [
                            part[:, half * group_width + i * share :][:, :share]
                            for part in (low_core, high_core)
                        ],
                        axis=1,
                    )
                    for half in range(2)
                ],
                axis=0,
            )
    step = 1
    while step < blk_count:
        odd = (b // step) % 2 == 1
        blocks = {d: jnp.where(odd, blocks[d ^ step], blocks[d]) for d in blocks}
        step *= 2
    total = jnp.concatenate([blocks[d] for d in range(blk_count)], axis=1)
    out_ref[...] = (total / denominator[...]).astype(out_ref.dtype)

    for copy in started:
        copy.wait_send()


def body(
    blk_count,
    virt_count,
    integrals,
    amplitudes,
    readers,
    row_slots,
    tile_mask,
    virt_energy,
    occ_energy,
    pair_first,
    pair_second,
):
    generated, tile_rows, width = integrals.shape
    panel_rows = amplitudes.shape[0]
    rows = virt_energy.shape[0]
    columns = blk_count * panel_rows
    groups = blk_count // 2
    levels = occ_energy.shape[0]
    lanes = generated * tile_rows
    packed_rows = rows // 2
    packed_width = 2 * panel_rows
    chunks = 2
    anywhere = pl.BlockSpec(memory_space=pl.ANY)
    return pl.pallas_call(
        functools.partial(kernel, blk_count, virt_count, chunks),
        out_shape=pltpu.VMEM((rows, columns), jnp.bfloat16),
        in_specs=[anywhere] * 9,
        out_specs=pl.BlockSpec(memory_space=pltpu.VMEM),
        scratch_shapes=[
            pltpu.VMEM((2 * lanes, width), jnp.bfloat16),
            pltpu.VMEM((columns // 2, width), jnp.bfloat16),
            pltpu.VMEM((groups, 2 * lanes, panel_rows), jnp.float32),
            pltpu.VMEM((groups, 2 * lanes, packed_width), jnp.float32),
            pltpu.VMEM((2, 8, lanes), jnp.int32),
            pltpu.VMEM((virt_count * rows, 2 * lanes), jnp.bfloat16),
            pltpu.VMEM((groups, virt_count * packed_rows, packed_width), jnp.float32),
            pltpu.VMEM((groups, virt_count, packed_rows, packed_width), jnp.float32),
            pltpu.VMEM((rows, columns), jnp.float32),
            pltpu.SMEM((generated,), jnp.int32),
            pltpu.SMEM((generated,), jnp.int32),
            pltpu.SMEM((blk_count, generated), jnp.int32),
            pltpu.VMEM((1, rows), jnp.float32),
            pltpu.VMEM((levels,), jnp.float32),
            pltpu.VMEM((1, columns), jnp.int32),
            pltpu.VMEM((1, columns), jnp.int32),
            pltpu.SemaphoreType.DMA((9,)),
            pltpu.SemaphoreType.DMA((3,)),
            pltpu.SemaphoreType.DMA((3,)),
            pltpu.SemaphoreType.DMA((blk_count, chunks)),
            pltpu.SemaphoreType.DMA((blk_count, chunks)),
            pltpu.SemaphoreType.DMA((2,)),
            pltpu.SemaphoreType.DMA((2,)),
            pltpu.SemaphoreType.DMA((blk_count, 4, chunks)),
            pltpu.SemaphoreType.DMA((blk_count, 4, chunks)),
            pltpu.SemaphoreType.DMA((groups, virt_count)),
            pltpu.SemaphoreType.DMA((groups, virt_count)),
        ],
        compiler_params=pltpu.CompilerParams(
            collective_id=0, has_side_effects=True, vmem_limit_bytes=60 * 1024 * 1024
        ),
        name="ladder",
    )(
        integrals.reshape(generated * tile_rows, width),
        amplitudes,
        readers,
        row_slots,
        tile_mask.T,
        virt_energy.reshape(1, rows),
        occ_energy,
        pair_first.reshape(1, columns),
        pair_second.reshape(1, columns),
    )


def solution(mesh):
    placed = (
        P(("blk", "virt"), None, None),
        P("blk", None),
        P(("blk", "virt")),
        P(("blk", "virt")),
        P(("blk", "virt"), None),
        P(("blk", "virt")),
        P(),
        P(),
        P(),
    )
    return jax.shard_map(
        functools.partial(body, mesh.shape["blk"], mesh.shape["virt"]),
        mesh=mesh,
        in_specs=placed,
        out_specs=P(("blk", "virt"), None),
        check_vma=False,
    )
```

```python
import functools

import jax
import jax.numpy as jnp
from jax import lax
from jax.experimental import pallas as pl
from jax.experimental.pallas import tpu as pltpu
from jax.sharding import PartitionSpec as P

MESH = pl.DeviceIdType.MESH


def flip(index, bits):
    step = 1
    while step <= bits:
        if bits & step:
            index = index + step * (1 - 2 * ((index // step) % 2))
        step *= 2
    return index


def panel_order(blk_count):
    order = [0, 3, 2, 1] if blk_count >= 4 else [0, 1]
    return order + list(range(4, blk_count))


def kernel(
    blk_count,
    virt_count,
    chunks,
    tiles_hbm,
    amp_hbm,
    readers_hbm,
    slots_hbm,
    mask_hbm,
    virt_hbm,
    occ_hbm,
    first_hbm,
    second_hbm,
    out_ref,
    tiles,
    amp,
    products,
    weights,
    goals,
    hot,
    partial,
    landed,
    denominator,
    readers,
    slots,
    mask,
    virt_energy,
    occ,
    first,
    second,
    local_sem,
    swap_send,
    swap_recv,
    far_send,
    far_recv,
    near_send,
    near_recv,
    plane_send,
    plane_recv,
    sum_send,
    sum_recv,
):
    b = lax.axis_index("blk")
    v = lax.axis_index("virt")
    core = v % 2
    spot = (v // 2) % 4
    generated = readers.shape[0]
    lanes = tiles.shape[0] // 2
    tile_rows = lanes // generated
    panel_rows, width = amp_hbm.shape
    share = panel_rows // 2
    rows = out_ref.shape[0]
    row_blocks = rows // tile_rows
    order = panel_order(blk_count)
    groups = blk_count // 2
    group_width = 2 * share
    packed_width = 2 * group_width
    packed_rows = rows // 2
    quarter = width // 4
    chunk = quarter // chunks
    sibling = (b, flip(v, 1))

    def keep(d):
        return pl.ds(order.index(d) * share, share)

    mine = pl.ds(pl.multiple_of(core * share, share), share)
    locals_ = [
        pltpu.make_async_copy(source, target, local_sem.at[index])
        for index, (source, target) in enumerate(
            (
                (readers_hbm, readers),
                (slots_hbm, slots),
                (mask_hbm, mask),
                (virt_hbm, virt_energy),
                (occ_hbm, occ),
                (first_hbm, first),
                (second_hbm, second),
                (amp_hbm.at[mine], amp.at[keep(0)]),
                (tiles_hbm, tiles.at[pl.ds(0, lanes)]),
            )
        )
    ]

    barrier = pltpu.get_barrier_semaphore()
    for d in range(1, blk_count):
        pl.semaphore_signal(barrier, inc=1, device_id=(flip(b, d), v), device_id_type=MESH)
    for d in range(1, virt_count):
        pl.semaphore_signal(barrier, inc=1, device_id=(b, flip(v, d)), device_id_type=MESH)
    for copy in locals_:
        copy.start()
    pl.semaphore_wait(barrier, blk_count + virt_count - 2)

    started = []

    def send(source, target, send_sem, recv_sem, device):
        copy = pltpu.make_async_remote_copy(
            source, target, send_sem, recv_sem, device_id=device, device_id_type=MESH
        )
        copy.start()
        started.append(copy)
        return copy

    def columns(spot_now, start, size):
        return pl.ds(pl.multiple_of(spot_now * quarter + start, size), size)

    far = {}
    for d in order[1:3] + order[4:]:
        if d == 1:
            continue
        for j in range(chunks):
            area = columns(spot, j * chunk, chunk)
            far[d, j] = send(
                amp_hbm.at[mine, area],
                amp.at[keep(d), area],
                far_send.at[d, j],
                far_recv.at[d, j],
                (flip(b, d), v),
            )
    near = {}
    for step in range(2):
        area = pl.ds(pl.multiple_of(flip(spot // 2, step) * 2 * quarter, quarter), 2 * quarter)
        near[step] = send(
            amp_hbm.at[mine, area],
            amp.at[keep(1), area],
            near_send.at[step],
            near_recv.at[step],
            (flip(b, 1), v),
        )
    tiles_swap = send(
        tiles_hbm, tiles.at[pl.ds(lanes, lanes)], swap_send.at[0], swap_recv.at[0], sibling
    )

    for copy in locals_[:7]:
        copy.wait()
    lane = lax.broadcasted_iota(jnp.int32, (1, lanes), 1)
    goal = jnp.zeros((1, lanes), jnp.int32)
    half_blocks = row_blocks // 2
    hot_rows = virt_count * packed_rows
    for t in range(generated):
        place = (
            (slots[t] // half_blocks) * hot_rows
            + readers[t] * packed_rows
            + (slots[t] % half_blocks) * tile_rows
        )
        goal = jnp.where(lane // tile_rows == t, place, goal)
    goal = goal + lane % tile_rows
    goals[0] = jnp.broadcast_to(goal, goals.shape[1:])
    goals_swap = send(goals.at[0], goals.at[1], swap_send.at[1], swap_recv.at[1], sibling)

    packed_lane = lax.broadcasted_iota(jnp.int32, (1, packed_width), 1)
    for g in range(groups):
        one, two = flip(b, order[2 * g]), flip(b, order[2 * g + 1])
        weights[g, :lanes] = jnp.concatenate(
            [
                jnp.broadcast_to(
                    jnp.where(packed_lane % group_width < share, mask[one, t], mask[two, t]).astype(
                        jnp.float32
                    ),
                    (tile_rows, packed_width),
                )
                for t in range(generated)
            ],
            axis=0,
        )
    weights_swap = send(
        weights.at[:, pl.ds(0, lanes)],
        weights.at[:, pl.ds(lanes, lanes)],
        swap_send.at[2],
        swap_recv.at[2],
        sibling,
    )

    def mark(part):
        row = lax.broadcasted_iota(jnp.int32, (2 * hot_rows, lanes), 0)
        hot[:, pl.ds(part * lanes, lanes)] = (
            (row == goals[part][0:1]).astype(jnp.float32).astype(jnp.bfloat16)
        )

    def energies():
        levels = occ.shape[0]
        occ_row = occ[...].reshape(1, levels)
        occ_high = occ_row.astype(jnp.bfloat16).astype(jnp.float32)
        occ_rest = occ_row - occ_high
        occ_mid = occ_rest.astype(jnp.bfloat16).astype(jnp.float32)
        occ_low = occ_rest - occ_mid
        term = lax.broadcasted_iota(jnp.int32, (8, levels), 0)
        occ_terms = jnp.where(
            term == 0, occ_high, jnp.where(term == 1, occ_mid, jnp.where(term == 2, occ_low, 0.0))
        ).astype(jnp.bfloat16)
        count = first.shape[1]
        level = lax.broadcasted_iota(jnp.int32, (levels, count), 0)

        def energy(pair_ref):
            chosen = (level == pair_ref[...]).astype(jnp.float32).astype(jnp.bfloat16)
            terms = jnp.dot(occ_terms, chosen, preferred_element_type=jnp.float32)
            return (terms[0:1] + terms[1:2]) + terms[2:3]

        diagonal = lax.broadcasted_iota(jnp.int32, (rows, rows), 0) == lax.broadcasted_iota(
            jnp.int32, (rows, rows), 1
        )
        virt_column = jnp.sum(jnp.where(diagonal, virt_energy[...], 0.0), axis=1, keepdims=True)
        denominator[...] = (virt_column - energy(first)) - energy(second)

    plane = {}

    def forward(d):
        for j in range(chunks):
            far[d, j].wait_recv()
            area = amp.at[keep(d), columns(spot, j * chunk, chunk)]
            for bits in (3, 1, 2):
                plane[d, bits, j] = send(
                    area,
                    area,
                    plane_send.at[d, bits, j],
                    plane_recv.at[d, bits, j],
                    (b, flip(v, 2 * bits)),
                )

    def multiply(g, step, parts=None):
        for j in range(chunks) if parts is None else parts:
            for d in order[2 * g : 2 * g + 2]:
                if d == 1 and step % 2 == 0 and j == 0:
                    near[step // 2].wait_recv()
                elif d > 1 and step:
                    plane[d, step, j].wait_recv()
        size = quarter if parts is None else chunk * len(parts)
        depth = columns(flip(spot, step), 0 if parts is None else parts[0] * chunk, size)
        term = lax.dot_general(
            tiles[:, depth],
            amp[pl.ds(g * group_width, group_width), depth],
            (((1,), (1,)), ((), ())),
            preferred_element_type=jnp.float32,
        )
        products[g] = term if step == 0 and (parts is None or parts[0] == 0) else products[g] + term

    sums = {}
    double_lane = lax.broadcasted_iota(jnp.int32, (1, 2 * packed_width), 1)

    def contract(g):
        product = products[g]
        product = jnp.concatenate([product, product], axis=1) * weights[g]
        high = product.astype(jnp.bfloat16)
        low = (product - high.astype(jnp.float32)).astype(jnp.bfloat16)
        both = jnp.dot(hot[...], jnp.concatenate([high, low], axis=1), preferred_element_type=jnp.float32)
        both = jnp.where(double_lane // group_width % 2 == 0, both[:hot_rows], both[hot_rows:])
        partial[g] = both[:, :packed_width] + both[:, packed_width:]
        for d in [6, 7, 2, 3, 4, 5] + list(range(8, virt_count)) + [1]:
            peer = flip(v, d)
            sums[g, d] = send(
                partial.at[g, pl.ds(pl.multiple_of(peer * packed_rows, packed_rows), packed_rows)],
                landed.at[g, d],
                sum_send.at[g, d],
                sum_recv.at[g, d],
                (b, peer),
            )

    mark(0)
    if blk_count >= 4:
        forward(3)
    goals_swap.wait_recv()
    mark(1)
    energies()
    locals_[7].wait()
    locals_[8].wait()
    tiles_swap.wait_recv()
    multiply(0, 0)
    if blk_count >= 4:
        forward(2)
        multiply(1, 0)
    for step in range(1, 4):
        multiply(0, step)
    weights_swap.wait_recv()
    contract(0)
    for g in range(1, groups):
        if g >= 2:
            forward(order[2 * g])
            forward(order[2 * g + 1])
            multiply(g, 0)
        for j in range(chunks):
            for step in range(1, 4):
                multiply(g, step, [j])
        contract(g)

    blocks = {}
    for g in range(groups):
        own = pl.ds(pl.multiple_of(v * packed_rows, packed_rows), packed_rows)
        same, other = partial[g, own, :], None
        for d in range(1, virt_count):
            sums[g, d].wait_recv()
            if d % 2 == 0:
                same = same + landed[g, d]
            else:
                other = landed[g, d] if other is None else other + landed[g, d]
        low_core = jnp.where(core == 0, same, other)
        high_core = jnp.where(core == 0, other, same)
        for i in range(2):
            blocks[order[2 * g + i]] = jnp.concatenate(
                [
                    jnp.concatenate(
                        [
                            part[:, half * group_width + i * share :][:, :share]
                            for part in (low_core, high_core)
                        ],
                        axis=1,
                    )
                    for half in range(2)
                ],
                axis=0,
            )
    step = 1
    while step < blk_count:
        odd = (b // step) % 2 == 1
        blocks = {d: jnp.where(odd, blocks[d ^ step], blocks[d]) for d in blocks}
        step *= 2
    total = jnp.concatenate([blocks[d] for d in range(blk_count)], axis=1)
    out_ref[...] = (total / denominator[...]).astype(out_ref.dtype)

    for copy in started:
        copy.wait_send()


def body(
    blk_count,
    virt_count,
    integrals,
    amplitudes,
    readers,
    row_slots,
    tile_mask,
    virt_energy,
    occ_energy,
    pair_first,
    pair_second,
):
    generated, tile_rows, width = integrals.shape
    panel_rows = amplitudes.shape[0]
    rows = virt_energy.shape[0]
    columns = blk_count * panel_rows
    groups = blk_count // 2
    levels = occ_energy.shape[0]
    lanes = generated * tile_rows
    packed_rows = rows // 2
    packed_width = 2 * panel_rows
    chunks = 2
    anywhere = pl.BlockSpec(memory_space=pl.ANY)
    return pl.pallas_call(
        functools.partial(kernel, blk_count, virt_count, chunks),
        out_shape=pltpu.VMEM((rows, columns), jnp.bfloat16),
        in_specs=[anywhere] * 9,
        out_specs=pl.BlockSpec(memory_space=pltpu.VMEM),
        scratch_shapes=[
            pltpu.VMEM((2 * lanes, width), jnp.bfloat16),
            pltpu.VMEM((columns // 2, width), jnp.bfloat16),
            pltpu.VMEM((groups, 2 * lanes, panel_rows), jnp.float32),
            pltpu.VMEM((groups, 2 * lanes, packed_width), jnp.float32),
            pltpu.VMEM((2, 8, lanes), jnp.int32),
            pltpu.VMEM((virt_count * rows, 2 * lanes), jnp.bfloat16),
            pltpu.VMEM((groups, virt_count * packed_rows, packed_width), jnp.float32),
            pltpu.VMEM((groups, virt_count, packed_rows, packed_width), jnp.float32),
            pltpu.VMEM((rows, columns), jnp.float32),
            pltpu.SMEM((generated,), jnp.int32),
            pltpu.SMEM((generated,), jnp.int32),
            pltpu.SMEM((blk_count, generated), jnp.int32),
            pltpu.VMEM((1, rows), jnp.float32),
            pltpu.VMEM((levels,), jnp.float32),
            pltpu.VMEM((1, columns), jnp.int32),
            pltpu.VMEM((1, columns), jnp.int32),
            pltpu.SemaphoreType.DMA((9,)),
            pltpu.SemaphoreType.DMA((3,)),
            pltpu.SemaphoreType.DMA((3,)),
            pltpu.SemaphoreType.DMA((blk_count, chunks)),
            pltpu.SemaphoreType.DMA((blk_count, chunks)),
            pltpu.SemaphoreType.DMA((2,)),
            pltpu.SemaphoreType.DMA((2,)),
            pltpu.SemaphoreType.DMA((blk_count, 4, chunks)),
            pltpu.SemaphoreType.DMA((blk_count, 4, chunks)),
            pltpu.SemaphoreType.DMA((groups, virt_count)),
            pltpu.SemaphoreType.DMA((groups, virt_count)),
        ],
        compiler_params=pltpu.CompilerParams(
            collective_id=0, has_side_effects=True, vmem_limit_bytes=60 * 1024 * 1024
        ),
        name="ladder",
    )(
        integrals.reshape(generated * tile_rows, width),
        amplitudes,
        readers,
        row_slots,
        tile_mask.T,
        virt_energy.reshape(1, rows),
        occ_energy,
        pair_first.reshape(1, columns),
        pair_second.reshape(1, columns),
    )


def solution(mesh):
    placed = (
        P(("blk", "virt"), None, None),
        P("blk", None),
        P(("blk", "virt")),
        P(("blk", "virt")),
        P(("blk", "virt"), None),
        P(("blk", "virt")),
        P(),
        P(),
        P(),
    )
    return jax.shard_map(
        functools.partial(body, mesh.shape["blk"], mesh.shape["virt"]),
        mesh=mesh,
        in_specs=placed,
        out_specs=P(("blk", "virt"), None),
        check_vma=False,
    )
```

```python
import functools

import jax
import jax.numpy as jnp
from jax import lax
from jax.experimental import pallas as pl
from jax.experimental.pallas import tpu as pltpu
from jax.sharding import PartitionSpec as P

MESH = pl.DeviceIdType.MESH


def flip(index, bits):
    step = 1
    while step <= bits:
        if bits & step:
            index = index + step * (1 - 2 * ((index // step) % 2))
        step *= 2
    return index


def panel_order(blk_count):
    order = [0, 3, 2, 1] if blk_count >= 4 else [0, 1]
    return order + list(range(4, blk_count))


def kernel(
    blk_count,
    virt_count,
    chunks,
    tiles_hbm,
    amp_hbm,
    readers_hbm,
    slots_hbm,
    mask_hbm,
    virt_hbm,
    occ_hbm,
    first_hbm,
    second_hbm,
    out_ref,
    tiles,
    amp,
    products,
    weights,
    goals,
    hot,
    partial,
    landed,
    denominator,
    readers,
    slots,
    mask,
    virt_energy,
    occ,
    first,
    second,
    local_sem,
    swap_send,
    swap_recv,
    far_send,
    far_recv,
    near_send,
    near_recv,
    plane_send,
    plane_recv,
    sum_send,
    sum_recv,
):
    b = lax.axis_index("blk")
    v = lax.axis_index("virt")
    core = v % 2
    spot = (v // 2) % 4
    generated = readers.shape[0]
    lanes = tiles.shape[0] // 2
    tile_rows = lanes // generated
    panel_rows, width = amp_hbm.shape
    share = panel_rows // 2
    rows = out_ref.shape[0]
    row_blocks = rows // tile_rows
    order = panel_order(blk_count)
    groups = blk_count // 2
    group_width = 2 * share
    packed_width = 2 * group_width
    packed_rows = rows // 2
    quarter = width // 4
    chunk = quarter // chunks
    peers = [6, 7, 2, 3, 4, 5] + list(range(8, virt_count)) + [1, 0]
    sibling = (b, flip(v, 1))

    def keep(d):
        return pl.ds(order.index(d) * share, share)

    mine = pl.ds(pl.multiple_of(core * share, share), share)
    locals_ = [
        pltpu.make_async_copy(source, target, local_sem.at[index])
        for index, (source, target) in enumerate(
            (
                (readers_hbm, readers),
                (slots_hbm, slots),
                (mask_hbm, mask),
                (virt_hbm, virt_energy),
                (occ_hbm, occ),
                (first_hbm, first),
                (second_hbm, second),
                (amp_hbm.at[mine], amp.at[keep(0)]),
                (tiles_hbm, tiles.at[pl.ds(0, lanes)]),
            )
        )
    ]

    barrier = pltpu.get_barrier_semaphore()
    for d in range(1, blk_count):
        pl.semaphore_signal(barrier, inc=1, device_id=(flip(b, d), v), device_id_type=MESH)
    for d in range(1, virt_count):
        pl.semaphore_signal(barrier, inc=1, device_id=(b, flip(v, d)), device_id_type=MESH)
    for copy in locals_:
        copy.start()
    pl.semaphore_wait(barrier, blk_count + virt_count - 2)

    started = []

    def send(source, target, send_sem, recv_sem, device):
        copy = pltpu.make_async_remote_copy(
            source, target, send_sem, recv_sem, device_id=device, device_id_type=MESH
        )
        copy.start()
        started.append(copy)
        return copy

    def columns(spot_now, start, size):
        return pl.ds(pl.multiple_of(spot_now * quarter + start, size), size)

    far = {}
    for d in order[1:3] + order[4:]:
        if d == 1:
            continue
        for j in range(chunks):
            area = columns(spot, j * chunk, chunk)
            far[d, j] = send(
                amp_hbm.at[mine, area],
                amp.at[keep(d), area],
                far_send.at[d, j],
                far_recv.at[d, j],
                (flip(b, d), v),
            )
    near = {}
    for step in range(2):
        area = pl.ds(pl.multiple_of(flip(spot // 2, step) * 2 * quarter, quarter), 2 * quarter)
        near[step] = send(
            amp_hbm.at[mine, area],
            amp.at[keep(1), area],
            near_send.at[step],
            near_recv.at[step],
            (flip(b, 1), v),
        )
    tiles_swap = send(
        tiles_hbm, tiles.at[pl.ds(lanes, lanes)], swap_send.at[0], swap_recv.at[0], sibling
    )

    for copy in locals_[:7]:
        copy.wait()
    lane = lax.broadcasted_iota(jnp.int32, (1, lanes), 1)
    goal = jnp.zeros((1, lanes), jnp.int32)
    for t in range(generated):
        place = readers[t] * rows + slots[t] * tile_rows
        goal = jnp.where(lane // tile_rows == t, place, goal)
    goal = goal + lane % tile_rows
    goals[0] = jnp.broadcast_to(goal, goals.shape[1:])
    goals_swap = send(goals.at[0], goals.at[1], swap_send.at[1], swap_recv.at[1], sibling)

    packed_lane = lax.broadcasted_iota(jnp.int32, (1, packed_width), 1)
    for g in range(groups):
        one, two = flip(b, order[2 * g]), flip(b, order[2 * g + 1])
        weights[g, :lanes] = jnp.concatenate(
            [
                jnp.broadcast_to(
                    jnp.where(packed_lane % group_width < share, mask[one, t], mask[two, t]).astype(
                        jnp.float32
                    ),
                    (tile_rows, packed_width),
                )
                for t in range(generated)
            ],
            axis=0,
        )
    weights_swap = send(
        weights.at[:, pl.ds(0, lanes)],
        weights.at[:, pl.ds(lanes, lanes)],
        swap_send.at[2],
        swap_recv.at[2],
        sibling,
    )

    def mark(part):
        row = lax.broadcasted_iota(jnp.int32, (rows, lanes), 0)
        relative = goals[part][0:1] ^ (v * rows)
        for index, d in enumerate(peers):
            hot[pl.ds(index * rows, rows), pl.ds(part * lanes, lanes)] = (
                (row == relative - d * rows).astype(jnp.float32).astype(jnp.bfloat16)
            )

    def energies():
        levels = occ.shape[0]
        occ_row = occ[...].reshape(1, levels)
        occ_high = occ_row.astype(jnp.bfloat16).astype(jnp.float32)
        occ_rest = occ_row - occ_high
        occ_mid = occ_rest.astype(jnp.bfloat16).astype(jnp.float32)
        occ_low = occ_rest - occ_mid
        term = lax.broadcasted_iota(jnp.int32, (8, levels), 0)
        occ_terms = jnp.where(
            term == 0, occ_high, jnp.where(term == 1, occ_mid, jnp.where(term == 2, occ_low, 0.0))
        ).astype(jnp.bfloat16)
        count = first.shape[1]
        level = lax.broadcasted_iota(jnp.int32, (levels, count), 0)

        def energy(pair_ref):
            chosen = (level == pair_ref[...]).astype(jnp.float32).astype(jnp.bfloat16)
            terms = jnp.dot(occ_terms, chosen, preferred_element_type=jnp.float32)
            return (terms[0:1] + terms[1:2]) + terms[2:3]

        diagonal = lax.broadcasted_iota(jnp.int32, (rows, rows), 0) == lax.broadcasted_iota(
            jnp.int32, (rows, rows), 1
        )
        virt_column = jnp.sum(jnp.where(diagonal, virt_energy[...], 0.0), axis=1, keepdims=True)
        denominator[...] = (virt_column - energy(first)) - energy(second)

    plane = {}

    def forward(d):
        for j in range(chunks):
            far[d, j].wait_recv()
            area = amp.at[keep(d), columns(spot, j * chunk, chunk)]
            for bits in (1, 2, 3):
                plane[d, bits, j] = send(
                    area,
                    area,
                    plane_send.at[d, bits, j],
                    plane_recv.at[d, bits, j],
                    (b, flip(v, 2 * bits)),
                )

    def multiply(g, step, parts=None):
        for j in range(chunks) if parts is None else parts:
            for d in order[2 * g : 2 * g + 2]:
                if d == 1 and step % 2 == 0 and j == 0:
                    near[step // 2].wait_recv()
                elif d > 1 and step:
                    plane[d, step, j].wait_recv()
        size = quarter if parts is None else chunk * len(parts)
        depth = columns(flip(spot, step), 0 if parts is None else parts[0] * chunk, size)
        term = lax.dot_general(
            tiles[:, depth],
            amp[pl.ds(g * group_width, group_width), depth],
            (((1,), (1,)), ((), ())),
            preferred_element_type=jnp.float32,
        )
        products[g] = term if step == 0 and (parts is None or parts[0] == 0) else products[g] + term

    sums = {}

    def contract(g):
        product = products[g]
        product = jnp.concatenate([product, product], axis=1) * weights[g]
        high = product.astype(jnp.bfloat16)
        low = (product - high.astype(jnp.float32)).astype(jnp.bfloat16)
        terms = jnp.concatenate([high, low], axis=1)
        for start in range(0, virt_count, 2):
            both = jnp.dot(
                hot[pl.ds(start * rows, 2 * rows)], terms, preferred_element_type=jnp.float32
            )
            both = both[:, :packed_width] + both[:, packed_width:]
            for index in range(start, start + 2):
                part = both[(index - start) * rows :][:rows]
                partial[g, index] = jnp.where(
                    packed_lane < group_width, part[:packed_rows], part[packed_rows:]
                )
                d = peers[index]
                if d:
                    sums[g, d] = send(
                        partial.at[g, index],
                        landed.at[g, d],
                        sum_send.at[g, d],
                        sum_recv.at[g, d],
                        (b, flip(v, d)),
                    )

    mark(0)
    if blk_count >= 4:
        forward(3)
    goals_swap.wait_recv()
    mark(1)
    energies()
    locals_[7].wait()
    locals_[8].wait()
    tiles_swap.wait_recv()
    multiply(0, 0)
    if blk_count >= 4:
        forward(2)
        multiply(1, 0)
    for step in range(1, 4):
        multiply(0, step)
    weights_swap.wait_recv()
    contract(0)
    for g in range(1, groups):
        if g >= 2:
            forward(order[2 * g])
            forward(order[2 * g + 1])
            multiply(g, 0)
        for j in range(chunks):
            for step in range(1, 4):
                multiply(g, step, [j])
        contract(g)

    for copy in started[: 1 - virt_count]:
        copy.wait_send()
    del started[: 1 - virt_count]
    blocks = {}
    for g in range(groups):
        same, other = partial[g, virt_count - 1], None
        for d in range(1, virt_count):
            sums[g, d].wait_recv()
            if d % 2 == 0:
                same = same + landed[g, d]
            else:
                other = landed[g, d] if other is None else other + landed[g, d]
        low_core = jnp.where(core == 0, same, other)
        high_core = jnp.where(core == 0, other, same)
        for i in range(2):
            blocks[order[2 * g + i]] = jnp.concatenate(
                [
                    jnp.concatenate(
                        [
                            part[:, half * group_width + i * share :][:, :share]
                            for part in (low_core, high_core)
                        ],
                        axis=1,
                    )
                    for half in range(2)
                ],
                axis=0,
            )
    step = 1
    while step < blk_count:
        odd = (b // step) % 2 == 1
        blocks = {d: jnp.where(odd, blocks[d ^ step], blocks[d]) for d in blocks}
        step *= 2
    total = jnp.concatenate([blocks[d] for d in range(blk_count)], axis=1)
    out_ref[...] = (total / denominator[...]).astype(out_ref.dtype)

    for copy in started:
        copy.wait_send()


def body(
    blk_count,
    virt_count,
    integrals,
    amplitudes,
    readers,
    row_slots,
    tile_mask,
    virt_energy,
    occ_energy,
    pair_first,
    pair_second,
):
    generated, tile_rows, width = integrals.shape
    panel_rows = amplitudes.shape[0]
    rows = virt_energy.shape[0]
    columns = blk_count * panel_rows
    groups = blk_count // 2
    levels = occ_energy.shape[0]
    lanes = generated * tile_rows
    packed_rows = rows // 2
    packed_width = 2 * panel_rows
    chunks = 2
    anywhere = pl.BlockSpec(memory_space=pl.ANY)
    return pl.pallas_call(
        functools.partial(kernel, blk_count, virt_count, chunks),
        out_shape=pltpu.VMEM((rows, columns), jnp.bfloat16),
        in_specs=[anywhere] * 9,
        out_specs=pl.BlockSpec(memory_space=pltpu.VMEM),
        scratch_shapes=[
            pltpu.VMEM((2 * lanes, width), jnp.bfloat16),
            pltpu.VMEM((columns // 2, width), jnp.bfloat16),
            pltpu.VMEM((groups, 2 * lanes, panel_rows), jnp.float32),
            pltpu.VMEM((groups, 2 * lanes, packed_width), jnp.float32),
            pltpu.VMEM((2, 8, lanes), jnp.int32),
            pltpu.VMEM((virt_count * rows, 2 * lanes), jnp.bfloat16),
            pltpu.VMEM((groups, virt_count, packed_rows, packed_width), jnp.float32),
            pltpu.VMEM((groups, virt_count, packed_rows, packed_width), jnp.float32),
            pltpu.VMEM((rows, columns), jnp.float32),
            pltpu.SMEM((generated,), jnp.int32),
            pltpu.SMEM((generated,), jnp.int32),
            pltpu.SMEM((blk_count, generated), jnp.int32),
            pltpu.VMEM((1, rows), jnp.float32),
            pltpu.VMEM((levels,), jnp.float32),
            pltpu.VMEM((1, columns), jnp.int32),
            pltpu.VMEM((1, columns), jnp.int32),
            pltpu.SemaphoreType.DMA((9,)),
            pltpu.SemaphoreType.DMA((3,)),
            pltpu.SemaphoreType.DMA((3,)),
            pltpu.SemaphoreType.DMA((blk_count, chunks)),
            pltpu.SemaphoreType.DMA((blk_count, chunks)),
            pltpu.SemaphoreType.DMA((2,)),
            pltpu.SemaphoreType.DMA((2,)),
            pltpu.SemaphoreType.DMA((blk_count, 4, chunks)),
            pltpu.SemaphoreType.DMA((blk_count, 4, chunks)),
            pltpu.SemaphoreType.DMA((groups, virt_count)),
            pltpu.SemaphoreType.DMA((groups, virt_count)),
        ],
        compiler_params=pltpu.CompilerParams(
            collective_id=0, has_side_effects=True, vmem_limit_bytes=60 * 1024 * 1024
        ),
        name="ladder",
    )(
        integrals.reshape(generated * tile_rows, width),
        amplitudes,
        readers,
        row_slots,
        tile_mask.T,
        virt_energy.reshape(1, rows),
        occ_energy,
        pair_first.reshape(1, columns),
        pair_second.reshape(1, columns),
    )


def solution(mesh):
    placed = (
        P(("blk", "virt"), None, None),
        P("blk", None),
        P(("blk", "virt")),
        P(("blk", "virt")),
        P(("blk", "virt"), None),
        P(("blk", "virt")),
        P(),
        P(),
        P(),
    )
    return jax.shard_map(
        functools.partial(body, mesh.shape["blk"], mesh.shape["virt"]),
        mesh=mesh,
        in_specs=placed,
        out_specs=P(("blk", "virt"), None),
        check_vma=False,
    )
```

```python
import functools

import jax
import jax.numpy as jnp
from jax import lax
from jax.experimental import pallas as pl
from jax.experimental.pallas import tpu as pltpu
from jax.sharding import PartitionSpec as P

MESH = pl.DeviceIdType.MESH


def flip(index, bits):
    step = 1
    while step <= bits:
        if bits & step:
            index = index + step * (1 - 2 * ((index // step) % 2))
        step *= 2
    return index


def panel_order(blk_count):
    order = [0, 3, 2, 1] if blk_count >= 4 else [0, 1]
    return order + list(range(4, blk_count))


def kernel(
    blk_count,
    virt_count,
    chunks,
    tiles_hbm,
    amp_hbm,
    readers_hbm,
    slots_hbm,
    mask_hbm,
    virt_hbm,
    occ_hbm,
    first_hbm,
    second_hbm,
    out_ref,
    tiles,
    amp,
    products,
    weights,
    goals,
    hot,
    partial,
    landed,
    denominator,
    readers,
    slots,
    mask,
    virt_energy,
    occ,
    first,
    second,
    local_sem,
    swap_send,
    swap_recv,
    far_send,
    far_recv,
    near_send,
    near_recv,
    plane_send,
    plane_recv,
    sum_send,
    sum_recv,
):
    b = lax.axis_index("blk")
    v = lax.axis_index("virt")
    core = v % 2
    spot = (v // 2) % 4
    generated = readers.shape[0]
    lanes = tiles.shape[0] // 2
    tile_rows = lanes // generated
    panel_rows, width = amp_hbm.shape
    share = panel_rows // 2
    rows = out_ref.shape[0]
    row_blocks = rows // tile_rows
    order = panel_order(blk_count)
    groups = blk_count // 2
    group_width = 2 * share
    packed_width = 2 * group_width
    packed_rows = rows // 2
    quarter = width // 4
    chunk = quarter // chunks
    peers = [6, 7, 2, 3, 4, 5] + list(range(8, virt_count)) + [1, 0]
    sibling = (b, flip(v, 1))

    def keep(d):
        return pl.ds(order.index(d) * share, share)

    mine = pl.ds(pl.multiple_of(core * share, share), share)
    locals_ = [
        pltpu.make_async_copy(source, target, local_sem.at[index])
        for index, (source, target) in enumerate(
            (
                (readers_hbm, readers),
                (slots_hbm, slots),
                (mask_hbm, mask),
                (virt_hbm, virt_energy),
                (occ_hbm, occ),
                (first_hbm, first),
                (second_hbm, second),
                (amp_hbm.at[mine], amp.at[keep(0)]),
                (tiles_hbm, tiles.at[pl.ds(0, lanes)]),
            )
        )
    ]

    barrier = pltpu.get_barrier_semaphore()
    for d in range(1, blk_count):
        pl.semaphore_signal(barrier, inc=1, device_id=(flip(b, d), v), device_id_type=MESH)
    for d in range(1, virt_count):
        pl.semaphore_signal(barrier, inc=1, device_id=(b, flip(v, d)), device_id_type=MESH)
    for copy in locals_:
        copy.start()
    pl.semaphore_wait(barrier, blk_count + virt_count - 2)

    started = []

    def send(source, target, send_sem, recv_sem, device):
        copy = pltpu.make_async_remote_copy(
            source, target, send_sem, recv_sem, device_id=device, device_id_type=MESH
        )
        copy.start()
        started.append(copy)
        return copy

    def columns(spot_now, start, size):
        return pl.ds(pl.multiple_of(spot_now * quarter + start, size), size)

    tiles_swap = send(
        tiles_hbm, tiles.at[pl.ds(lanes, lanes)], swap_send.at[0], swap_recv.at[0], sibling
    )

    far = {}
    for d in order[1:3] + order[4:]:
        if d == 1:
            continue
        for j in range(chunks):
            area = columns(spot, j * chunk, chunk)
            far[d, j] = send(
                amp_hbm.at[mine, area],
                amp.at[keep(d), area],
                far_send.at[d, j],
                far_recv.at[d, j],
                (flip(b, d), v),
            )
    near = {}
    for step in range(2):
        area = pl.ds(pl.multiple_of(flip(spot // 2, step) * 2 * quarter, quarter), 2 * quarter)
        near[step] = send(
            amp_hbm.at[mine, area],
            amp.at[keep(1), area],
            near_send.at[step],
            near_recv.at[step],
            (flip(b, 1), v),
        )
    for copy in locals_[:7]:
        copy.wait()
    lane = lax.broadcasted_iota(jnp.int32, (1, lanes), 1)
    goal = jnp.zeros((1, lanes), jnp.int32)
    for t in range(generated):
        place = readers[t] * rows + slots[t] * tile_rows
        goal = jnp.where(lane // tile_rows == t, place, goal)
    goal = goal + lane % tile_rows
    goals[0] = jnp.broadcast_to(goal, goals.shape[1:])
    goals_swap = send(goals.at[0], goals.at[1], swap_send.at[1], swap_recv.at[1], sibling)

    packed_lane = lax.broadcasted_iota(jnp.int32, (1, packed_width), 1)
    for g in range(groups):
        one, two = flip(b, order[2 * g]), flip(b, order[2 * g + 1])
        weights[g, :lanes] = jnp.concatenate(
            [
                jnp.broadcast_to(
                    jnp.where(packed_lane % group_width < share, mask[one, t], mask[two, t]).astype(
                        jnp.float32
                    ),
                    (tile_rows, packed_width),
                )
                for t in range(generated)
            ],
            axis=0,
        )
    weights_swap = send(
        weights.at[:, pl.ds(0, lanes)],
        weights.at[:, pl.ds(lanes, lanes)],
        swap_send.at[2],
        swap_recv.at[2],
        sibling,
    )

    def mark(part):
        row = lax.broadcasted_iota(jnp.int32, (rows, lanes), 0)
        relative = goals[part][0:1] ^ (v * rows)
        for index, d in enumerate(peers):
            hot[pl.ds(index * rows, rows), pl.ds(part * lanes, lanes)] = (
                (row == relative - d * rows).astype(jnp.float32).astype(jnp.bfloat16)
            )

    def energies():
        levels = occ.shape[0]
        occ_row = occ[...].reshape(1, levels)
        occ_high = occ_row.astype(jnp.bfloat16).astype(jnp.float32)
        occ_rest = occ_row - occ_high
        occ_mid = occ_rest.astype(jnp.bfloat16).astype(jnp.float32)
        occ_low = occ_rest - occ_mid
        term = lax.broadcasted_iota(jnp.int32, (8, levels), 0)
        occ_terms = jnp.where(
            term == 0, occ_high, jnp.where(term == 1, occ_mid, jnp.where(term == 2, occ_low, 0.0))
        ).astype(jnp.bfloat16)
        count = first.shape[1]
        level = lax.broadcasted_iota(jnp.int32, (levels, count), 0)

        def energy(pair_ref):
            chosen = (level == pair_ref[...]).astype(jnp.float32).astype(jnp.bfloat16)
            terms = jnp.dot(occ_terms, chosen, preferred_element_type=jnp.float32)
            return (terms[0:1] + terms[1:2]) + terms[2:3]

        diagonal = lax.broadcasted_iota(jnp.int32, (rows, rows), 0) == lax.broadcasted_iota(
            jnp.int32, (rows, rows), 1
        )
        virt_column = jnp.sum(jnp.where(diagonal, virt_energy[...], 0.0), axis=1, keepdims=True)
        denominator[...] = (virt_column - energy(first)) - energy(second)

    plane = {}

    def forward(d):
        for j in range(chunks):
            far[d, j].wait_recv()
            area = amp.at[keep(d), columns(spot, j * chunk, chunk)]
            for bits in (1, 2, 3):
                plane[d, bits, j] = send(
                    area,
                    area,
                    plane_send.at[d, bits, j],
                    plane_recv.at[d, bits, j],
                    (b, flip(v, 2 * bits)),
                )

    def multiply(g, step, parts=None):
        for j in range(chunks) if parts is None else parts:
            for d in order[2 * g : 2 * g + 2]:
                if d == 1 and step % 2 == 0 and j == 0:
                    near[step // 2].wait_recv()
                elif d > 1 and step:
                    plane[d, step, j].wait_recv()
        size = quarter if parts is None else chunk * len(parts)
        depth = columns(flip(spot, step), 0 if parts is None else parts[0] * chunk, size)
        term = lax.dot_general(
            tiles[:, depth],
            amp[pl.ds(g * group_width, group_width), depth],
            (((1,), (1,)), ((), ())),
            preferred_element_type=jnp.float32,
        )
        products[g] = term if step == 0 and (parts is None or parts[0] == 0) else products[g] + term

    sums = {}

    def contract(g):
        product = products[g]
        product = jnp.concatenate([product, product], axis=1) * weights[g]
        high = product.astype(jnp.bfloat16)
        low = (product - high.astype(jnp.float32)).astype(jnp.bfloat16)
        terms = jnp.concatenate([high, low], axis=1)
        for start in range(0, virt_count, 2):
            both = jnp.dot(
                hot[pl.ds(start * rows, 2 * rows)], terms, preferred_element_type=jnp.float32
            )
            both = both[:, :packed_width] + both[:, packed_width:]
            for index in range(start, start + 2):
                part = both[(index - start) * rows :][:rows]
                partial[g, index] = jnp.where(
                    packed_lane < group_width, part[:packed_rows], part[packed_rows:]
                )
                d = peers[index]
                if d:
                    sums[g, d] = send(
                        partial.at[g, index],
                        landed.at[g, d],
                        sum_send.at[g, d],
                        sum_recv.at[g, d],
                        (b, flip(v, d)),
                    )

    mark(0)
    if blk_count >= 4:
        forward(3)
    energies()
    locals_[7].wait()
    locals_[8].wait()
    tiles_swap.wait_recv()
    multiply(0, 0)
    if blk_count >= 4:
        forward(2)
        multiply(1, 0)
    for step in range(1, 4):
        multiply(0, step)
    goals_swap.wait_recv()
    mark(1)
    weights_swap.wait_recv()
    contract(0)
    for g in range(1, groups):
        if g >= 2:
            forward(order[2 * g])
            forward(order[2 * g + 1])
            multiply(g, 0)
        for j in range(chunks):
            for step in range(1, 4):
                multiply(g, step, [j])
        contract(g)

    for copy in started[: 1 - virt_count]:
        copy.wait_send()
    del started[: 1 - virt_count]
    blocks = {}
    for g in range(groups):
        same, other = partial[g, virt_count - 1], None
        for d in range(1, virt_count):
            sums[g, d].wait_recv()
            if d % 2 == 0:
                same = same + landed[g, d]
            else:
                other = landed[g, d] if other is None else other + landed[g, d]
        low_core = jnp.where(core == 0, same, other)
        high_core = jnp.where(core == 0, other, same)
        for i in range(2):
            blocks[order[2 * g + i]] = jnp.concatenate(
                [
                    jnp.concatenate(
                        [
                            part[:, half * group_width + i * share :][:, :share]
                            for part in (low_core, high_core)
                        ],
                        axis=1,
                    )
                    for half in range(2)
                ],
                axis=0,
            )
    step = 1
    while step < blk_count:
        odd = (b // step) % 2 == 1
        blocks = {d: jnp.where(odd, blocks[d ^ step], blocks[d]) for d in blocks}
        step *= 2
    total = jnp.concatenate([blocks[d] for d in range(blk_count)], axis=1)
    out_ref[...] = (total / denominator[...]).astype(out_ref.dtype)

    for copy in started:
        copy.wait_send()


def body(
    blk_count,
    virt_count,
    integrals,
    amplitudes,
    readers,
    row_slots,
    tile_mask,
    virt_energy,
    occ_energy,
    pair_first,
    pair_second,
):
    generated, tile_rows, width = integrals.shape
    panel_rows = amplitudes.shape[0]
    rows = virt_energy.shape[0]
    columns = blk_count * panel_rows
    groups = blk_count // 2
    levels = occ_energy.shape[0]
    lanes = generated * tile_rows
    packed_rows = rows // 2
    packed_width = 2 * panel_rows
    chunks = 2
    anywhere = pl.BlockSpec(memory_space=pl.ANY)
    return pl.pallas_call(
        functools.partial(kernel, blk_count, virt_count, chunks),
        out_shape=pltpu.VMEM((rows, columns), jnp.bfloat16),
        in_specs=[anywhere] * 9,
        out_specs=pl.BlockSpec(memory_space=pltpu.VMEM),
        scratch_shapes=[
            pltpu.VMEM((2 * lanes, width), jnp.bfloat16),
            pltpu.VMEM((columns // 2, width), jnp.bfloat16),
            pltpu.VMEM((groups, 2 * lanes, panel_rows), jnp.float32),
            pltpu.VMEM((groups, 2 * lanes, packed_width), jnp.float32),
            pltpu.VMEM((2, 8, lanes), jnp.int32),
            pltpu.VMEM((virt_count * rows, 2 * lanes), jnp.bfloat16),
            pltpu.VMEM((groups, virt_count, packed_rows, packed_width), jnp.float32),
            pltpu.VMEM((groups, virt_count, packed_rows, packed_width), jnp.float32),
            pltpu.VMEM((rows, columns), jnp.float32),
            pltpu.SMEM((generated,), jnp.int32),
            pltpu.SMEM((generated,), jnp.int32),
            pltpu.SMEM((blk_count, generated), jnp.int32),
            pltpu.VMEM((1, rows), jnp.float32),
            pltpu.VMEM((levels,), jnp.float32),
            pltpu.VMEM((1, columns), jnp.int32),
            pltpu.VMEM((1, columns), jnp.int32),
            pltpu.SemaphoreType.DMA((9,)),
            pltpu.SemaphoreType.DMA((3,)),
            pltpu.SemaphoreType.DMA((3,)),
            pltpu.SemaphoreType.DMA((blk_count, chunks)),
            pltpu.SemaphoreType.DMA((blk_count, chunks)),
            pltpu.SemaphoreType.DMA((2,)),
            pltpu.SemaphoreType.DMA((2,)),
            pltpu.SemaphoreType.DMA((blk_count, 4, chunks)),
            pltpu.SemaphoreType.DMA((blk_count, 4, chunks)),
            pltpu.SemaphoreType.DMA((groups, virt_count)),
            pltpu.SemaphoreType.DMA((groups, virt_count)),
        ],
        compiler_params=pltpu.CompilerParams(
            collective_id=0, has_side_effects=True, vmem_limit_bytes=60 * 1024 * 1024
        ),
        name="ladder",
    )(
        integrals.reshape(generated * tile_rows, width),
        amplitudes,
        readers,
        row_slots,
        tile_mask.T,
        virt_energy.reshape(1, rows),
        occ_energy,
        pair_first.reshape(1, columns),
        pair_second.reshape(1, columns),
    )


def solution(mesh):
    placed = (
        P(("blk", "virt"), None, None),
        P("blk", None),
        P(("blk", "virt")),
        P(("blk", "virt")),
        P(("blk", "virt"), None),
        P(("blk", "virt")),
        P(),
        P(),
        P(),
    )
    return jax.shard_map(
        functools.partial(body, mesh.shape["blk"], mesh.shape["virt"]),
        mesh=mesh,
        in_specs=placed,
        out_specs=P(("blk", "virt"), None),
        check_vma=False,
    )
```

```python
import functools

import jax
import jax.numpy as jnp
from jax import lax
from jax.experimental import pallas as pl
from jax.experimental.pallas import tpu as pltpu
from jax.sharding import PartitionSpec as P

MESH = pl.DeviceIdType.MESH


def flip(index, bits):
    step = 1
    while step <= bits:
        if bits & step:
            index = index + step * (1 - 2 * ((index // step) % 2))
        step *= 2
    return index


def panel_order(blk_count):
    order = [0, 3, 2, 1] if blk_count >= 4 else [0, 1]
    return order + list(range(4, blk_count))


def kernel(
    blk_count,
    virt_count,
    chunks,
    tiles_hbm,
    amp_hbm,
    readers_hbm,
    slots_hbm,
    mask_hbm,
    virt_hbm,
    occ_hbm,
    first_hbm,
    second_hbm,
    out_ref,
    tiles,
    amp,
    products,
    weights,
    goals,
    hot,
    partial,
    landed,
    denominator,
    readers,
    slots,
    mask,
    virt_energy,
    occ,
    first,
    second,
    local_sem,
    swap_send,
    swap_recv,
    far_send,
    far_recv,
    near_send,
    near_recv,
    plane_send,
    plane_recv,
    sum_send,
    sum_recv,
):
    b = lax.axis_index("blk")
    v = lax.axis_index("virt")
    core = v % 2
    spot = (v // 2) % 4
    generated = readers.shape[0]
    lanes = tiles.shape[0] // 2
    tile_rows = lanes // generated
    panel_rows, width = amp_hbm.shape
    share = panel_rows // 2
    rows = out_ref.shape[0]
    row_blocks = rows // tile_rows
    order = panel_order(blk_count)
    groups = blk_count // 2
    group_width = 2 * share
    packed_width = 2 * group_width
    packed_rows = rows // 2
    quarter = width // 4
    chunk = quarter // chunks
    peers = [6, 7, 2, 3, 4, 5] + list(range(8, virt_count)) + [1, 0]
    sibling = (b, flip(v, 1))

    def keep(d):
        return pl.ds(order.index(d) * share, share)

    mine = pl.ds(pl.multiple_of(core * share, share), share)
    locals_ = [
        pltpu.make_async_copy(source, target, local_sem.at[index])
        for index, (source, target) in enumerate(
            (
                (readers_hbm, readers),
                (slots_hbm, slots),
                (mask_hbm, mask),
                (virt_hbm, virt_energy),
                (occ_hbm, occ),
                (first_hbm, first),
                (second_hbm, second),
                (amp_hbm.at[mine], amp.at[keep(0)]),
                (tiles_hbm, tiles.at[pl.ds(0, lanes)]),
            )
        )
    ]

    barrier = pltpu.get_barrier_semaphore()
    for d in range(1, blk_count):
        pl.semaphore_signal(barrier, inc=1, device_id=(flip(b, d), v), device_id_type=MESH)
    for d in range(1, virt_count):
        pl.semaphore_signal(barrier, inc=1, device_id=(b, flip(v, d)), device_id_type=MESH)
    for copy in locals_[:7]:
        copy.start()
    pl.semaphore_wait(barrier, blk_count + virt_count - 2)

    started = []

    def send(source, target, send_sem, recv_sem, device):
        copy = pltpu.make_async_remote_copy(
            source, target, send_sem, recv_sem, device_id=device, device_id_type=MESH
        )
        copy.start()
        started.append(copy)
        return copy

    def columns(spot_now, start, size):
        return pl.ds(pl.multiple_of(spot_now * quarter + start, size), size)

    tiles_swap = send(
        tiles_hbm, tiles.at[pl.ds(lanes, lanes)], swap_send.at[0], swap_recv.at[0], sibling
    )

    far = {}
    for d in order[1:3] + order[4:]:
        if d == 1:
            continue
        for j in range(chunks):
            area = columns(spot, j * chunk, chunk)
            far[d, j] = send(
                amp_hbm.at[mine, area],
                amp.at[keep(d), area],
                far_send.at[d, j],
                far_recv.at[d, j],
                (flip(b, d), v),
            )
    near = {}
    for step in range(2):
        area = pl.ds(pl.multiple_of(flip(spot // 2, step) * 2 * quarter, quarter), 2 * quarter)
        near[step] = send(
            amp_hbm.at[mine, area],
            amp.at[keep(1), area],
            near_send.at[step],
            near_recv.at[step],
            (flip(b, 1), v),
        )
    for copy in locals_[7:]:
        copy.start()
    for copy in locals_[:7]:
        copy.wait()
    lane = lax.broadcasted_iota(jnp.int32, (1, lanes), 1)
    goal = jnp.zeros((1, lanes), jnp.int32)
    for t in range(generated):
        place = readers[t] * rows + slots[t] * tile_rows
        goal = jnp.where(lane // tile_rows == t, place, goal)
    goal = goal + lane % tile_rows
    goals[0] = jnp.broadcast_to(goal, goals.shape[1:])
    goals_swap = send(goals.at[0], goals.at[1], swap_send.at[1], swap_recv.at[1], sibling)

    packed_lane = lax.broadcasted_iota(jnp.int32, (1, packed_width), 1)
    for g in range(groups):
        one, two = flip(b, order[2 * g]), flip(b, order[2 * g + 1])
        weights[g, :lanes] = jnp.concatenate(
            [
                jnp.broadcast_to(
                    jnp.where(packed_lane % group_width < share, mask[one, t], mask[two, t]).astype(
                        jnp.float32
                    ),
                    (tile_rows, packed_width),
                )
                for t in range(generated)
            ],
            axis=0,
        )
    weights_swap = send(
        weights.at[:, pl.ds(0, lanes)],
        weights.at[:, pl.ds(lanes, lanes)],
        swap_send.at[2],
        swap_recv.at[2],
        sibling,
    )

    def mark(part):
        row = lax.broadcasted_iota(jnp.int32, (rows, lanes), 0)
        relative = goals[part][0:1] ^ (v * rows)
        for index, d in enumerate(peers):
            hot[pl.ds(index * rows, rows), pl.ds(part * lanes, lanes)] = (
                (row == relative - d * rows).astype(jnp.float32).astype(jnp.bfloat16)
            )

    def energies():
        levels = occ.shape[0]
        occ_row = occ[...].reshape(1, levels)
        occ_high = occ_row.astype(jnp.bfloat16).astype(jnp.float32)
        occ_rest = occ_row - occ_high
        occ_mid = occ_rest.astype(jnp.bfloat16).astype(jnp.float32)
        occ_low = occ_rest - occ_mid
        term = lax.broadcasted_iota(jnp.int32, (8, levels), 0)
        occ_terms = jnp.where(
            term == 0, occ_high, jnp.where(term == 1, occ_mid, jnp.where(term == 2, occ_low, 0.0))
        ).astype(jnp.bfloat16)
        count = first.shape[1]
        level = lax.broadcasted_iota(jnp.int32, (levels, count), 0)

        def energy(pair_ref):
            chosen = (level == pair_ref[...]).astype(jnp.float32).astype(jnp.bfloat16)
            terms = jnp.dot(occ_terms, chosen, preferred_element_type=jnp.float32)
            return (terms[0:1] + terms[1:2]) + terms[2:3]

        diagonal = lax.broadcasted_iota(jnp.int32, (rows, rows), 0) == lax.broadcasted_iota(
            jnp.int32, (rows, rows), 1
        )
        virt_column = jnp.sum(jnp.where(diagonal, virt_energy[...], 0.0), axis=1, keepdims=True)
        denominator[...] = (virt_column - energy(first)) - energy(second)

    plane = {}

    def forward(d):
        for j in range(chunks):
            far[d, j].wait_recv()
            area = amp.at[keep(d), columns(spot, j * chunk, chunk)]
            for bits in (1, 2, 3):
                plane[d, bits, j] = send(
                    area,
                    area,
                    plane_send.at[d, bits, j],
                    plane_recv.at[d, bits, j],
                    (b, flip(v, 2 * bits)),
                )

    def multiply(g, step, parts=None):
        for j in range(chunks) if parts is None else parts:
            for d in order[2 * g : 2 * g + 2]:
                if d == 1 and step % 2 == 0 and j == 0:
                    near[step // 2].wait_recv()
                elif d > 1 and step:
                    plane[d, step, j].wait_recv()
        size = quarter if parts is None else chunk * len(parts)
        depth = columns(flip(spot, step), 0 if parts is None else parts[0] * chunk, size)
        term = lax.dot_general(
            tiles[:, depth],
            amp[pl.ds(g * group_width, group_width), depth],
            (((1,), (1,)), ((), ())),
            preferred_element_type=jnp.float32,
        )
        products[g] = term if step == 0 and (parts is None or parts[0] == 0) else products[g] + term

    sums = {}

    def contract(g):
        product = products[g]
        product = jnp.concatenate([product, product], axis=1) * weights[g]
        high = product.astype(jnp.bfloat16)
        low = (product - high.astype(jnp.float32)).astype(jnp.bfloat16)
        terms = jnp.concatenate([high, low], axis=1)
        for start in range(0, virt_count, 2):
            both = jnp.dot(
                hot[pl.ds(start * rows, 2 * rows)], terms, preferred_element_type=jnp.float32
            )
            both = both[:, :packed_width] + both[:, packed_width:]
            for index in range(start, start + 2):
                part = both[(index - start) * rows :][:rows]
                partial[g, index] = jnp.where(
                    packed_lane < group_width, part[:packed_rows], part[packed_rows:]
                )
                d = peers[index]
                if d:
                    sums[g, d] = send(
                        partial.at[g, index],
                        landed.at[g, d],
                        sum_send.at[g, d],
                        sum_recv.at[g, d],
                        (b, flip(v, d)),
                    )

    mark(0)
    if blk_count >= 4:
        forward(3)
    goals_swap.wait_recv()
    mark(1)
    energies()
    locals_[7].wait()
    locals_[8].wait()
    tiles_swap.wait_recv()
    multiply(0, 0)
    if blk_count >= 4:
        forward(2)
        multiply(1, 0)
    for step in range(1, 4):
        multiply(0, step)
    weights_swap.wait_recv()
    contract(0)
    for g in range(1, groups):
        if g >= 2:
            forward(order[2 * g])
            forward(order[2 * g + 1])
            multiply(g, 0)
        for j in range(chunks):
            for step in range(1, 4):
                multiply(g, step, [j])
        contract(g)

    for copy in started[: 1 - virt_count]:
        copy.wait_send()
    del started[: 1 - virt_count]
    blocks = {}
    for g in range(groups):
        same, other = partial[g, virt_count - 1], None
        for d in range(1, virt_count):
            sums[g, d].wait_recv()
            if d % 2 == 0:
                same = same + landed[g, d]
            else:
                other = landed[g, d] if other is None else other + landed[g, d]
        low_core = jnp.where(core == 0, same, other)
        high_core = jnp.where(core == 0, other, same)
        for i in range(2):
            blocks[order[2 * g + i]] = jnp.concatenate(
                [
                    jnp.concatenate(
                        [
                            part[:, half * group_width + i * share :][:, :share]
                            for part in (low_core, high_core)
                        ],
                        axis=1,
                    )
                    for half in range(2)
                ],
                axis=0,
            )
    step = 1
    while step < blk_count:
        odd = (b // step) % 2 == 1
        blocks = {d: jnp.where(odd, blocks[d ^ step], blocks[d]) for d in blocks}
        step *= 2
    total = jnp.concatenate([blocks[d] for d in range(blk_count)], axis=1)
    out_ref[...] = (total / denominator[...]).astype(out_ref.dtype)

    for copy in started:
        copy.wait_send()


def body(
    blk_count,
    virt_count,
    integrals,
    amplitudes,
    readers,
    row_slots,
    tile_mask,
    virt_energy,
    occ_energy,
    pair_first,
    pair_second,
):
    generated, tile_rows, width = integrals.shape
    panel_rows = amplitudes.shape[0]
    rows = virt_energy.shape[0]
    columns = blk_count * panel_rows
    groups = blk_count // 2
    levels = occ_energy.shape[0]
    lanes = generated * tile_rows
    packed_rows = rows // 2
    packed_width = 2 * panel_rows
    chunks = 2
    anywhere = pl.BlockSpec(memory_space=pl.ANY)
    return pl.pallas_call(
        functools.partial(kernel, blk_count, virt_count, chunks),
        out_shape=pltpu.VMEM((rows, columns), jnp.bfloat16),
        in_specs=[anywhere] * 9,
        out_specs=pl.BlockSpec(memory_space=pltpu.VMEM),
        scratch_shapes=[
            pltpu.VMEM((2 * lanes, width), jnp.bfloat16),
            pltpu.VMEM((columns // 2, width), jnp.bfloat16),
            pltpu.VMEM((groups, 2 * lanes, panel_rows), jnp.float32),
            pltpu.VMEM((groups, 2 * lanes, packed_width), jnp.float32),
            pltpu.VMEM((2, 8, lanes), jnp.int32),
            pltpu.VMEM((virt_count * rows, 2 * lanes), jnp.bfloat16),
            pltpu.VMEM((groups, virt_count, packed_rows, packed_width), jnp.float32),
            pltpu.VMEM((groups, virt_count, packed_rows, packed_width), jnp.float32),
            pltpu.VMEM((rows, columns), jnp.float32),
            pltpu.SMEM((generated,), jnp.int32),
            pltpu.SMEM((generated,), jnp.int32),
            pltpu.SMEM((blk_count, generated), jnp.int32),
            pltpu.VMEM((1, rows), jnp.float32),
            pltpu.VMEM((levels,), jnp.float32),
            pltpu.VMEM((1, columns), jnp.int32),
            pltpu.VMEM((1, columns), jnp.int32),
            pltpu.SemaphoreType.DMA((9,)),
            pltpu.SemaphoreType.DMA((3,)),
            pltpu.SemaphoreType.DMA((3,)),
            pltpu.SemaphoreType.DMA((blk_count, chunks)),
            pltpu.SemaphoreType.DMA((blk_count, chunks)),
            pltpu.SemaphoreType.DMA((2,)),
            pltpu.SemaphoreType.DMA((2,)),
            pltpu.SemaphoreType.DMA((blk_count, 4, chunks)),
            pltpu.SemaphoreType.DMA((blk_count, 4, chunks)),
            pltpu.SemaphoreType.DMA((groups, virt_count)),
            pltpu.SemaphoreType.DMA((groups, virt_count)),
        ],
        compiler_params=pltpu.CompilerParams(
            collective_id=0, has_side_effects=True, vmem_limit_bytes=60 * 1024 * 1024
        ),
        name="ladder",
    )(
        integrals.reshape(generated * tile_rows, width),
        amplitudes,
        readers,
        row_slots,
        tile_mask.T,
        virt_energy.reshape(1, rows),
        occ_energy,
        pair_first.reshape(1, columns),
        pair_second.reshape(1, columns),
    )


def solution(mesh):
    placed = (
        P(("blk", "virt"), None, None),
        P("blk", None),
        P(("blk", "virt")),
        P(("blk", "virt")),
        P(("blk", "virt"), None),
        P(("blk", "virt")),
        P(),
        P(),
        P(),
    )
    return jax.shard_map(
        functools.partial(body, mesh.shape["blk"], mesh.shape["virt"]),
        mesh=mesh,
        in_specs=placed,
        out_specs=P(("blk", "virt"), None),
        check_vma=False,
    )
```
